768 devices in a mesh: grp: 48 (over y, z_lo, core), dp: 16 (over z_hi, x).
Axes of the slice: x: 4, y: 8, z: 12 (z_hi: 4, z_lo: 3; z = z_hi * 3 + z_lo), core: 2. Of those that a mesh axis runs over, the one named last changes fastest.
Arguments:
- vis_features: bfloat16 [49152, 3200], P(('grp', 'dp')), may hold values from -6 to 6
- vis_gain: float32 [3200], replicated, may hold values from 0.1 to 1.9
- proj_weight: bfloat16 [3200, 8192], P(None, 'dp'), may hold values from -0.109375 to 0.109375
- proj_bias: float32 [8192], P('dp'), may hold values from -3 to 3
- text_embed: bfloat16 [73728, 8192], P('grp', 'dp'), may hold values from -6 to 6
- out_gain: float32 [8192], P('dp'), may hold values from 0.1 to 1.9
- image_counts: int32 [768], P(('grp', 'dp')), may hold values from 1 to 4, as said below
- owner_block: int32 [3072], P(('grp', 'dp')), may hold values from 0 to 47, as said below
- offsets: int32 [3072], P(('grp', 'dp')), may hold values from 0 to 1520, as said below
Outputs:
- hidden: bfloat16 [73728, 8192], P('grp', 'dp')
The draws below stay inside these ranges and needn't reach their ends.
Inputs may be any that keep to these rules, and one draw needn't show every extreme that they name: The live images of a device are its first image_counts slots; some device holds 4 in every draw. `owner_block`: among the image slots of one index of grp (live or not), at most 2 name the same owner, and in every such block some owner is named by exactly 2. `offsets`: the image slots that name one owner (live or not) cover disjoint runs of 16 positions inside its 1536 positions.
All inputs are finite; a program needn't handle non-finite values.
Results may differ from the reference program's by a relative error of at most 0.0043.
Values may be sent and summed in bfloat16 or wider, within the bound.
A program may use at most 64 MiB of HBM per device.

```python
import jax
import jax.numpy as jnp
from jax import lax

V = 3200
D = 8192
PATCH = 16
IMG_CAP = 4
CAP = 2
LEN = 1536
IMAGES = 3072
TOKENS = 73728


def layout_tables(key):
    blocks = LEN // (CAP * PATCH)
    block_slots = IMAGES // blocks

    def one_block(block_key):
        key_order, key_seats, key_slots = jax.random.split(block_key, 3)
        dest_order = jax.random.permutation(key_order, blocks)
        other_seats = jax.random.permutation(key_seats, (blocks - 1) * CAP)[:block_slots - CAP]
        seat_dest = jnp.concatenate([jnp.full((CAP,), dest_order[0], dtype=jnp.int32), dest_order[1 + other_seats // CAP].astype(jnp.int32)])
        slot_order = jax.random.permutation(key_slots, block_slots)
        return seat_dest[slot_order]
    block_keys = jax.random.split(jax.random.fold_in(key, 7), blocks)
    owners = jax.vmap(one_block)(block_keys).reshape(-1).astype(jnp.int32)
    onehot = (owners[:, None] == jnp.arange(blocks, dtype=jnp.int32)[None, :]).astype(jnp.int32)
    running = jnp.cumsum(onehot, axis=0) - onehot
    rank_in = jnp.sum(running * onehot, axis=1)
    per_owner = jnp.sum(onehot, axis=0)[owners]
    spacing = (LEN - per_owner * PATCH) // (per_owner + 1)
    starts = rank_in * PATCH + (rank_in + 1) * spacing
    return (owners, starts.astype(jnp.int32))


def draw_owner_block(key, part):
    return layout_tables(key)[0]


def draw_offsets(key, part):
    return layout_tables(key)[1]


def draw_image_counts(key, part):
    devices = IMAGES // IMG_CAP
    key_pick, key_chosen = jax.random.split(jax.random.fold_in(key, 11))
    draw_pick = jax.random.randint(key_pick, (devices,), 0, 4)
    counts = jnp.where(draw_pick == 0, IMG_CAP, 1 + draw_pick % max(1, IMG_CAP // 2))
    chosen = jax.random.randint(key_chosen, (), 0, devices)
    counts = jnp.where(jnp.arange(devices) == chosen, IMG_CAP, counts)
    return jnp.clip(counts, 1, IMG_CAP).astype(jnp.int32)


def block_scale(own_key, extent, shards, smallest, high):
    def one(axis_at, shards_of):
        draws = jax.random.uniform(jax.random.fold_in(jax.random.fold_in(own_key, 6), axis_at), (shards_of,), jnp.float32, smallest / len(shards), high / len(shards))
        return jnp.repeat(jnp.exp(draws), extent[axis_at] // shards_of).reshape((-1,) + (1,) * (len(extent) - axis_at - 1))

    factor_of = one(*shards[0])
    for cut in shards[1:]:
        factor_of = factor_of * one(*cut)
    return factor_of


def bell_draw(rng, extent, spread, bound, pieces=(), kind=jnp.bfloat16):
    result = jax.random.normal(rng, extent, jnp.float32) * spread
    if len(pieces) > 0:
        result = block_scale(rng, extent, pieces, -0.22, 0.18) * result
    return jnp.clip(result, min=-bound, max=bound).astype(kind)


def setup_inputs(seed: int = 0) -> dict:
    splits = jax.random.split(jax.random.key(seed), 10)
    vis_features = bell_draw(splits[0], (IMAGES * PATCH, V), 1.0, 6.0, ((0, 768),))
    vis_gain = jnp.clip(1.0 + 0.18 * jax.random.normal(splits[1], (V,), jnp.float32), 0.1, 1.9)
    proj_weight = bell_draw(splits[2], (V, D), V ** -0.5, 0.109375, ((1, 16),))
    proj_bias = bell_draw(splits[3], (D,), 0.5, 3.0, ((0, 16),), jnp.float32)
    text_embed = bell_draw(splits[4], (TOKENS, D), 1.0, 6.0, ((0, 48), (1, 16)))
    out_gain = jnp.clip(1.0 + 0.18 * jax.random.normal(splits[5], (D,), jnp.float32), 0.1, 1.9)
    image_counts = draw_image_counts(jax.random.fold_in(splits[9], 71), 0)
    owner_block = draw_owner_block(jax.random.fold_in(splits[9], 71), 0)
    offsets = draw_offsets(jax.random.fold_in(splits[9], 71), 0)
    return {"vis_features": vis_features, "vis_gain": vis_gain, "proj_weight": proj_weight, "proj_bias": proj_bias, "text_embed": text_embed, "out_gain": out_gain, "image_counts": image_counts, "owner_block": owner_block, "offsets": offsets}


def reference(vis_features, vis_gain, proj_weight, proj_bias, text_embed, out_gain, image_counts, owner_block, offsets):
    vis_rows = vis_features.astype(jnp.float32)
    normed = (vis_rows * lax.rsqrt(lax.optimization_barrier(jnp.mean(vis_rows * vis_rows, axis=-1, keepdims=True)) + 1e-06) * vis_gain).astype(jnp.bfloat16)
    projected = (jnp.dot(normed, proj_weight, preferred_element_type=jnp.float32) + proj_bias).astype(jnp.bfloat16)
    images = owner_block.shape[0]
    slot_index = jnp.arange(images, dtype=jnp.int32) % IMG_CAP
    is_live = slot_index < jnp.repeat(image_counts, IMG_CAP)
    row_start = owner_block * LEN + offsets
    target_rows = row_start[:, None] + jnp.arange(PATCH, dtype=jnp.int32)[None, :]
    target_rows = jnp.where(is_live[:, None], target_rows, TOKENS).reshape(-1).astype(jnp.int32)
    merged = text_embed.at[target_rows].set(projected, mode='drop')
    merged_f = merged.astype(jnp.float32)
    hidden = merged_f * lax.rsqrt(lax.optimization_barrier(jnp.mean(merged_f * merged_f, axis=-1, keepdims=True)) + 1e-05) * out_gain
    return hidden.astype(jnp.bfloat16)
```

```python
import functools

import jax
import jax.numpy as jnp
from jax import lax
from jax.experimental import pallas as pl
from jax.experimental.pallas import tpu as pltpu
from jax.sharding import PartitionSpec as P

MESH = pl.DeviceIdType.MESH
PATCH = 16
CAP = 2
DP_X = 4
DP_Z = 4
PIECES = 4
LANES = 128


def row_sums(values):
    f = values.astype(jnp.float32)
    sq = f * f
    part = sq[:, :LANES]
    for c in range(1, values.shape[1] // LANES):
        part = part + sq[:, c * LANES : (c + 1) * LANES]
    return jnp.sum(part.T, axis=0, keepdims=True)


def spread(row, columns):
    square = jnp.broadcast_to(row, (LANES, LANES)).T
    return jnp.concatenate([square] * (columns // LANES), axis=1)


def exchange_kernel(
    dims,
    vis_ref,
    vgain_ref,
    w_hbm,
    bias_ref,
    text_hbm,
    ogain_ref,
    count_ref,
    owner_ref,
    offset_ref,
    arrived_ref,
    places_ref,
    thid_hbm,
    gather,
    w_ref,
    text_ref,
    thid_ref,
    proj,
    outbox,
    meta,
    table,
    table_s,
    tstat,
    pstat,
    local_sem,
    zs_sem,
    zr_sem,
    xs_sem,
    xr_sem,
    g_sem,
    ms_sem,
    mr_sem,
    ts_sem,
    tr_sem,
    ps_sem,
    pr_sem,
    os_sem,
    or_sem,
    as_sem,
    ar_sem,
):
    groups, ranks, features = dims
    grp = lax.axis_index("grp")
    dp = lax.axis_index("dp")
    zi, xi = dp // DP_X, dp % DP_X
    up, down, zop = (zi + 1) % DP_Z, (zi + 3) % DP_Z, (zi + 2) % DP_Z
    right, left, xop = (xi + 1) % DP_X, (xi + 3) % DP_X, (xi + 2) % DP_X
    planes = (zi, down, up, zop)

    def remote(src, dst, ssem, rsem, **where):
        return pltpu.make_async_remote_copy(
            src_ref=src, dst_ref=dst, send_sem=ssem, recv_sem=rsem, device_id=where, device_id_type=MESH
        )

    w_copy = pltpu.make_async_copy(w_hbm, w_ref, local_sem.at[0])
    text_copy = pltpu.make_async_copy(text_hbm, text_ref, local_sem.at[1])
    w_copy.start()
    text_copy.start()

    barrier = pltpu.get_barrier_semaphore()

    @pl.loop(1, ranks)
    def _(k):
        pl.semaphore_signal(barrier, inc=1, device_id={"dp": (dp + k) % ranks}, device_id_type=MESH)

    @pl.loop(1, groups)
    def _(k):
        pl.semaphore_signal(barrier, inc=1, device_id={"grp": (grp + k) % groups}, device_id_type=MESH)

    f = vis_ref[...].astype(jnp.float32)
    normed = (
        f * lax.rsqrt(jnp.mean(f * f, axis=-1, keepdims=True) + 1e-06) * vgain_ref[...]
    ).astype(jnp.bfloat16)
    gather[dp] = normed.reshape(gather.shape[1:])

    lane = lax.broadcasted_iota(jnp.int32, (8, LANES), 1)
    owners = jnp.zeros((8, LANES), jnp.int32)
    places = jnp.zeros((8, LANES), jnp.int32)
    slots = owner_ref.shape[0]
    for j in range(slots):
        mine = lane == dp * slots + j
        owners = jnp.where(mine, owner_ref[j], owners)
        live = jnp.full((8, LANES), count_ref[0], jnp.int32) > j
        places = jnp.where(mine & live, offset_ref[j] + 1, places)
    meta[dp, 0] = owners
    meta[dp, 1] = places

    pl.semaphore_wait(barrier, ranks - 1 + groups - 1)

    def z_copy(plane, s, target, sem):
        piece = gather.at[plane * DP_X + xi, s]
        return remote(piece, piece, sem, g_sem.at[plane * DP_X + xi, s], dp=target * DP_X + xi)

    def x_copy(plane, source, s, target, sem):
        piece = gather.at[plane * DP_X + source, s]
        return remote(piece, piece, sem, g_sem.at[plane * DP_X + source, s], dp=zi * DP_X + target)

    sends = []

    def go(copy):
        copy.start()
        sends.append(copy)

    def send_x(q, s):
        go(x_copy(planes[q], xi, s, right, xs_sem.at[q, 0, s]))
        go(x_copy(planes[q], xi, s, left, xs_sem.at[q, 1, s]))

    def arrived_x(q, source, s):
        x_copy(planes[q], source, s, right, xs_sem.at[q, 0, s]).wait_recv()

    def relay_x(q, s):
        if s % 2 == 0:
            arrived_x(q, left, s)
            go(x_copy(planes[q], left, s, right, xr_sem.at[q, s]))
        else:
            arrived_x(q, right, s)
            go(x_copy(planes[q], right, s, left, xr_sem.at[q, s]))

    def finish_x(q):
        for s in range(PIECES):
            arrived_x(q, right if s % 2 == 0 else left, s)
            arrived_x(q, xop, s)

    def arrived_z(q, s):
        z_copy(planes[q], s, up, zs_sem.at[0, s]).wait_recv()

    for s in range(PIECES):
        go(z_copy(zi, s, up, zs_sem.at[0, s]))
        go(z_copy(zi, s, down, zs_sem.at[1, s]))
        send_x(0, s)

    def to_ranks(buffer, ssem, rsem, act):
        @pl.loop(1, ranks)
        def _(k):
            peer = (dp + k) % ranks
            act(remote(buffer.at[dp], buffer.at[dp], ssem.at[peer], rsem.at[dp], dp=peer))

    def from_ranks(buffer, ssem, rsem):
        @pl.loop(1, ranks)
        def _(k):
            peer = (dp + k) % ranks
            remote(buffer.at[peer], buffer.at[peer], ssem.at[peer], rsem.at[peer], dp=peer).wait_recv()

    start = lambda copy: copy.start()
    wait_send = lambda copy: copy.wait_send()

    to_ranks(meta, ms_sem, mr_sem, start)

    text_copy.wait()
    text_blocks = text_ref.shape[0]

    @pl.loop(0, text_blocks)
    def _(b):
        tstat[dp, b] = row_sums(text_ref[b])

    to_ranks(tstat, ts_sem, tr_sem, start)

    for s in range(PIECES):
        relay_x(0, s)

    def project(q):
        plane = planes[q]
        rows = gather[pl.ds(plane * DP_X, DP_X)]
        rows = rows.reshape(DP_X * PIECES * PATCH, rows.shape[-1])
        out = jnp.dot(rows, w_ref[...], preferred_element_type=jnp.float32) + bias_ref[...]
        out = out.astype(jnp.bfloat16)
        images = DP_X * PIECES
        proj[pl.ds(plane * images, images)] = out.reshape(images, PATCH, out.shape[-1])
        for b in range(2):
            pstat[dp, plane * 2 + b] = row_sums(out[b * LANES : (b + 1) * LANES])

    def tables():
        from_ranks(meta, ms_sem, mr_sem)
        owners = meta[0, 0]
        places = meta[0, 1]
        for r in range(1, ranks):
            owners = owners + meta[r, 0]
            places = places + meta[r, 1]
        owner_row = owners[:1][None]
        place_row = places[:1][None]
        shape = (groups, 1, LANES)
        slot = lax.broadcasted_iota(jnp.int32, shape, 2)
        group = lax.broadcasted_iota(jnp.int32, shape, 0)
        named = (owner_row == group) & (slot < ranks * slots)
        first = jnp.min(jnp.where(named, slot, LANES), axis=2, keepdims=True)
        last = jnp.max(jnp.where(named, slot, -1), axis=2, keepdims=True)
        at_first = jnp.max(jnp.where(named & (slot == first), place_row, 0), axis=2, keepdims=True)
        at_last = jnp.max(
            jnp.where(named & (slot == last) & (slot != first), place_row, 0), axis=2, keepdims=True
        )
        first = jnp.minimum(first, ranks * slots - 1)
        last = jnp.maximum(last, 0)
        values = jnp.where(slot == 0, at_first - 1, at_last - 1)
        values = jnp.where(slot == 2, first, values)
        values = jnp.where(slot == 3, last, values)
        table[...] = values

    def table_copy(peer):
        return remote(table.at[peer], places_ref.at[grp], os_sem.at[peer], or_sem.at[grp], grp=peer)

    def out_copy(peer):
        return remote(outbox.at[peer], arrived_ref.at[grp], as_sem.at[peer], ar_sem.at[grp], grp=peer)

    def to_groups(make, act):
        @pl.loop(1, groups)
        def _(k):
            act(make((grp + k) % groups))

    def text_hidden():
        from_ranks(tstat, ts_sem, tr_sem)

        @pl.loop(0, text_blocks)
        def _(b):
            total = tstat[0, b]
            for r in range(1, ranks):
                total = total + tstat[r, b]
            inverse = lax.rsqrt(total / features + 1e-05)
            rows = text_ref[b].astype(jnp.float32)
            rows = rows * spread(inverse, rows.shape[1]) * ogain_ref[...]
            thid_ref[b] = rows.astype(jnp.bfloat16)

    thid_copy = pltpu.make_async_copy(thid_ref, thid_hbm, local_sem.at[2])
    table_smem = pltpu.make_async_copy(table, table_s, local_sem.at[3])
    place_own = pltpu.make_async_copy(table.at[grp], places_ref.at[grp], local_sem.at[4])
    out_own = pltpu.make_async_copy(outbox.at[grp], arrived_ref.at[grp], local_sem.at[5])

    w_copy.wait()
    for s in range(PIECES):
        arrived_z(1, s)
        if s % 2 == 0:
            go(z_copy(down, s, up, zr_sem.at[s]))
        send_x(1, s)
        arrived_z(2, s)
        if s % 2 == 1:
            go(z_copy(up, s, down, zr_sem.at[s]))
        send_x(2, s)
        if s >= 1:
            relay_x(1, s - 1)
            relay_x(2, s - 1)
        if s == 0:
            tables()
            table_smem.start()
            place_own.start()
            to_groups(table_copy, start)
        if s == 1:
            finish_x(0)
            project(0)
        if s == 2:
            text_hidden()
            thid_copy.start()

    for s in range(PIECES):
        arrived_z(3, s)
        send_x(3, s)
        if s == 1:
            relay_x(1, PIECES - 1)
            relay_x(2, PIECES - 1)
            relay_x(3, 0)
        if s == 2:
            finish_x(1)
            project(1)
            relay_x(3, 1)
    finish_x(2)
    project(2)
    relay_x(3, 2)
    relay_x(3, 3)
    finish_x(3)
    project(3)

    to_ranks(pstat, ps_sem, pr_sem, start)
    table_smem.wait()
    from_ranks(pstat, ps_sem, pr_sem)

    @pl.loop(0, pstat.shape[1])
    def _(b):
        total = pstat[0, b]
        for r in range(1, ranks):
            total = total + pstat[r, b]
        inverse = lax.rsqrt(total / features + 1e-05)
        images = LANES // PATCH
        rows = proj[pl.ds(b * images, images)]
        shape = rows.shape
        rows = rows.reshape(LANES, shape[-1]).astype(jnp.float32)
        rows = rows * spread(inverse, shape[-1]) * ogain_ref[...]
        proj[pl.ds(b * images, images)] = rows.astype(jnp.bfloat16).reshape(shape)

    @pl.loop(0, groups)
    def _(o):
        for r in range(CAP):
            outbox[o, r] = proj[table_s[o, 0, CAP + r]]

    to_groups(out_copy, start)
    out_own.start()

    to_ranks(meta, ms_sem, mr_sem, wait_send)
    to_ranks(tstat, ts_sem, tr_sem, wait_send)
    to_ranks(pstat, ps_sem, pr_sem, wait_send)
    to_groups(table_copy, wait_send)
    for copy in sends:
        copy.wait_send()
    thid_copy.wait()
    place_own.wait()

    @pl.loop(1, groups)
    def _(k):
        peer = (grp + k) % groups
        remote(table.at[peer], places_ref.at[peer], os_sem.at[peer], or_sem.at[peer], grp=peer).wait_recv()

    @pl.loop(1, groups)
    def _(k):
        peer = (grp + k) % groups
        remote(outbox.at[peer], arrived_ref.at[peer], as_sem.at[peer], ar_sem.at[peer], grp=peer).wait()

    out_own.wait()


def overlay_kernel(places_ref, thid_ref, arrived_ref, out_ref, rows):
    chunks = rows.shape[0]
    for c in range(chunks):
        rows[c] = thid_ref[:, c * LANES : (c + 1) * LANES].astype(jnp.float32)

    @pl.loop(0, arrived_ref.shape[0])
    def _(g):
        for r in range(CAP):
            at = places_ref[g, 0, r]

            @pl.when(at >= 0)
            def _():
                image = arrived_ref[g, r].astype(jnp.float32)
                for c in range(chunks):
                    rows[c, pl.ds(at, PATCH), :] = image[:, c * LANES : (c + 1) * LANES]

    for c in range(chunks):
        out_ref[:, c * LANES : (c + 1) * LANES] = rows[c].astype(jnp.bfloat16)


def on_device(
    ranks,
    vis_features,
    vis_gain,
    proj_weight,
    proj_bias,
    text_embed,
    out_gain,
    image_counts,
    owner_block,
    offsets,
):
    groups = lax.axis_size("grp")
    width, columns = proj_weight.shape
    seq_len = text_embed.shape[0]
    slots = ranks * owner_block.shape[0]
    text_blocks = seq_len // LANES
    stat_blocks = slots * PATCH // LANES
    bf16, f32, i32 = jnp.bfloat16, jnp.float32, jnp.int32
    vmem = pl.BlockSpec(memory_space=pltpu.VMEM)
    smem = pl.BlockSpec(memory_space=pltpu.SMEM)
    hbm = pl.BlockSpec(memory_space=pl.ANY)
    dma = pltpu.SemaphoreType.DMA
    arrived, places, thid = pl.pallas_call(
        functools.partial(exchange_kernel, (groups, ranks, ranks * columns)),
        out_shape=(
            jax.ShapeDtypeStruct((groups, CAP, PATCH, columns), bf16),
            jax.ShapeDtypeStruct((groups, 1, LANES), i32),
            jax.ShapeDtypeStruct((text_blocks, LANES, columns), bf16),
        ),
        in_specs=[vmem, vmem, hbm, vmem, hbm, vmem, smem, smem, smem],
        out_specs=(hbm, hbm, hbm),
        scratch_shapes=[
            pltpu.VMEM((ranks, PIECES, PATCH, width), bf16),
            pltpu.VMEM((width, columns), bf16),
            pltpu.VMEM((text_blocks, LANES, columns), bf16),
            pltpu.VMEM((text_blocks, LANES, columns), bf16),
            pltpu.VMEM((slots, PATCH, columns), bf16),
            pltpu.VMEM((groups, CAP, PATCH, columns), bf16),
            pltpu.VMEM((ranks, 2, 8, LANES), i32),
            pltpu.VMEM((groups, 1, LANES), i32),
            pltpu.SMEM((groups, 1, LANES), i32),
            pltpu.VMEM((ranks, text_blocks, 1, LANES), f32),
            pltpu.VMEM((ranks, stat_blocks, 1, LANES), f32),
            dma((6,)),
            dma((2, PIECES)),
            dma((PIECES,)),
            dma((DP_Z, 2, PIECES)),
            dma((DP_Z, PIECES)),
            dma((ranks, PIECES)),
            dma((ranks,)),
            dma((ranks,)),
            dma((ranks,)),
            dma((ranks,)),
            dma((ranks,)),
            dma((ranks,)),
            dma((groups,)),
            dma((groups,)),
            dma((groups,)),
            dma((groups,)),
        ],
        compiler_params=pltpu.CompilerParams(
            collective_id=0, has_side_effects=True, vmem_limit_bytes=48 << 20
        ),
        name="exchange",
    )(
        vis_features,
        vis_gain.reshape(1, width),
        proj_weight,
        proj_bias.reshape(1, columns),
        text_embed.reshape(text_blocks, LANES, columns),
        out_gain.reshape(1, columns),
        image_counts,
        owner_block,
        offsets,
    )
    return pl.pallas_call(
        overlay_kernel,
        out_shape=jax.ShapeDtypeStruct((seq_len, columns), bf16),
        in_specs=[smem, vmem, vmem],
        out_specs=vmem,
        scratch_shapes=[pltpu.VMEM((columns // LANES, seq_len, LANES), f32)],
        compiler_params=pltpu.CompilerParams(vmem_limit_bytes=32 << 20),
        name="overlay",
    )(places, thid.reshape(seq_len, columns), arrived)


def solution(mesh):
    return jax.shard_map(
        functools.partial(on_device, mesh.shape["dp"]),
        mesh=mesh,
        in_specs=(
            P(("grp", "dp"), None),
            P(),
            P(None, "dp"),
            P("dp"),
            P("grp", "dp"),
            P("dp"),
            P(("grp", "dp")),
            P(("grp", "dp")),
            P(("grp", "dp")),
        ),
        out_specs=P("grp", "dp"),
        check_vma=False,
    )
```

```python
import functools

import jax
import jax.numpy as jnp
from jax import lax
from jax.experimental import pallas as pl
from jax.experimental.pallas import tpu as pltpu
from jax.sharding import PartitionSpec as P

MESH = pl.DeviceIdType.MESH
PATCH = 16
CAP = 2
DP_X = 4
DP_Z = 4
PIECES = 4
Z_LO = 3
CORES = 2
SPAN = 2048
LANES = 128


def row_sums(values):
    f = values.astype(jnp.float32)
    sq = f * f
    part = sq[:, :LANES]
    for c in range(1, values.shape[1] // LANES):
        part = part + sq[:, c * LANES : (c + 1) * LANES]
    return jnp.sum(part.T, axis=0, keepdims=True)


def spread(row, columns):
    square = jnp.broadcast_to(row, (LANES, LANES)).T
    return jnp.concatenate([square] * (columns // LANES), axis=1)


def arrival_order(piece=2.2, latency=1.6, ahead=3):
    free = dict.fromkeys("UDRL", 0.0)
    now = 0.0
    pending = {}
    order = []

    def send(link, key):
        free[link] = max(free[link], now) + piece
        pending[key] = free[link] + latency

    def own(s):
        order.append(("own", s))
        for d in "UD":
            send(d, ("z", d, 1, s))

    def across(q, s):
        for d in "RL":
            send(d, ("x", q, d, 1, s))

    for s in range(PIECES):
        if s < ahead:
            own(s)
        order.append(("ownx", s))
        across(0, s)
    following = ahead
    count = [0] * DP_Z
    tasks = [(0.0, "tstat", 2.0), (8.0, "tables", 1.5), (9.0, "text2", 0.3), (20.0, "text3", 2.5)]
    while pending or tasks:
        here = [k for k, t in pending.items() if t <= now]
        ready = [t for t in tasks if t[0] <= now]
        if not here and ready:
            tasks.remove(ready[0])
            order.append(("task", ready[0][1]))
            now += ready[0][2]
            continue
        if not here:
            now = min([*pending.values(), *[t[0] for t in tasks]])
            continue
        key = min(here, key=lambda k: pending[k])
        del pending[key]
        order.append(key)
        now += 0.06
        if key[0] == "z":
            _, d, age, s = key
            if goes_on(d, age, s):
                send(d, ("z", d, age + 1, s))
            if age % Z_LO == 0:
                across(plane_of(d, age), s)
            if age == 1 and d == "D" and following < PIECES:
                own(following)
                following += 1
        else:
            _, q, d, age, s = key
            if age == 1 and s % 2 == (d == "L"):
                send(d, ("x", q, d, 2, s))
            count[q] += 1
            if count[q] == (DP_X - 1) * PIECES:
                tasks.append((now, q, 3.0))
    return order


def goes_on(d, age, s):
    return age < Z_LO or (age < 2 * Z_LO and s % 2 == (d == "D"))


def plane_of(d, age):
    return 3 if age == 2 * Z_LO else 1 if d == "U" else 2


def exchange_kernel(
    dims,
    vis_hbm,
    vgain_hbm,
    w_hbm,
    bias_hbm,
    text_hbm,
    ogain_hbm,
    count_hbm,
    owner_hbm,
    offset_hbm,
    arrived_ref,
    places_ref,
    thid_hbm,
    vis_ref,
    vgain_ref,
    bias_ref,
    ogain_ref,
    count_ref,
    owner_ref,
    offset_ref,
    gather,
    passing,
    w_ref,
    text_ref,
    thid_ref,
    proj,
    outbox,
    meta,
    table,
    table_s,
    tstat_x,
    tstat_z,
    pstat_x,
    pstat_z,
    local_sem,
    zs_sem,
    zg_sem,
    xs_sem,
    xr_sem,
    g_sem,
    ms_sem,
    mr_sem,
    ts_sem,
    tr_sem,
    ps_sem,
    pr_sem,
    os_sem,
    or_sem,
    as_sem,
    ar_sem,
):
    groups, ranks, features = dims
    grp = lax.axis_index("grp")
    dp = lax.axis_index("dp")
    zi, xi = dp // DP_X, dp % DP_X
    core, z_lo, y = grp % CORES, grp // CORES % Z_LO, grp // CORES // Z_LO
    z = zi * Z_LO + z_lo
    z_ring = DP_Z * Z_LO
    planes = (zi, (zi + 3) % DP_Z, (zi + 1) % DP_Z, (zi + 2) % DP_Z)
    x_next = {"R": (xi + 1) % DP_X, "L": (xi + 3) % DP_X}
    x_from = {"R": (xi + 3) % DP_X, "L": (xi + 1) % DP_X}
    x_far = (xi + 2) % DP_X

    def z_device(at):
        return {"grp": (y * Z_LO + at % Z_LO) * CORES + core, "dp": at // Z_LO * DP_X + xi}

    z_next = {"U": z_device((z + 1) % z_ring), "D": z_device((z + z_ring - 1) % z_ring)}

    def remote(src, dst, ssem, rsem, **where):
        return pltpu.make_async_remote_copy(
            src_ref=src, dst_ref=dst, send_sem=ssem, recv_sem=rsem, device_id=where, device_id_type=MESH
        )

    loads = [
        pltpu.make_async_copy(src, dst, local_sem.at[4 + n])
        for n, (src, dst) in enumerate(
            [
                (vis_hbm, vis_ref),
                (vgain_hbm, vgain_ref),
                (owner_hbm, owner_ref),
                (offset_hbm, offset_ref),
                (count_hbm, count_ref),
                (bias_hbm, bias_ref),
                (ogain_hbm, ogain_ref),
                (text_hbm, text_ref),
                (w_hbm, w_ref),
            ]
        )
    ]
    for copy in loads:
        copy.start()

    barrier = pltpu.get_barrier_semaphore()

    for d in "UD":
        pl.semaphore_signal(barrier, inc=1, device_id=z_next[d], device_id_type=MESH)

    @pl.loop(1, ranks)
    def _(k):
        pl.semaphore_signal(barrier, inc=1, device_id={"dp": (dp + k) % ranks}, device_id_type=MESH)

    @pl.loop(1, groups)
    def _(k):
        pl.semaphore_signal(barrier, inc=1, device_id={"grp": (grp + k) % groups}, device_id_type=MESH)

    for copy in loads[:7]:
        copy.wait()
    f = vis_ref[...].astype(jnp.float32)
    normed = (
        f * lax.rsqrt(jnp.mean(f * f, axis=-1, keepdims=True) + 1e-06) * vgain_ref[...]
    ).astype(jnp.bfloat16)
    gather[dp] = normed.reshape(gather.shape[1:])

    lane = lax.broadcasted_iota(jnp.int32, (1, LANES), 1)
    packed = jnp.zeros((1, LANES), jnp.int32)
    slots = owner_ref.shape[0]
    for j in range(slots):
        live = jnp.full((1, LANES), count_ref[0], jnp.int32) > j
        value = owner_ref[j] * SPAN + jnp.where(live, offset_ref[j] + 1, 0)
        packed = jnp.where(lane == dp * slots + j, value, packed)
    meta[dp] = packed

    pl.semaphore_wait(barrier, ranks - 1 + groups - 1 + 2)

    def z_source(d, age):
        return ((z + z_ring - age if d == "U" else z + age) % z_ring) // Z_LO

    def z_slot(d, age, s, arriving):
        if age % Z_LO == 0:
            return gather.at[z_source(d, age) * DP_X + xi, s]
        return passing.at["UD".index(d), age - 1 - age // Z_LO, s]

    def z_copy(d, age, s):
        if age % Z_LO == 0:
            target = gather.at[z_source(d, age - 1) * DP_X + xi, s]
        else:
            target = passing.at["UD".index(d), age - 1 - age // Z_LO, s]
        n = "UD".index(d)
        return remote(
            z_slot(d, age - 1, s, False), target, zs_sem.at[n, age - 1, s], zg_sem.at[n, age - 1, s], **z_next[d]
        )

    def z_arrival(d, age, s):
        n = "UD".index(d)
        piece = z_slot(d, age, s, True)
        return remote(piece, piece, zs_sem.at[n, age - 1, s], zg_sem.at[n, age - 1, s], **z_next[d])

    def x_copy(q, source, d, s, sem):
        place = planes[q] * DP_X + source
        piece = gather.at[place, s]
        return remote(piece, piece, sem, g_sem.at[place, s], dp=zi * DP_X + x_next[d])

    sends = []

    def go(copy):
        copy.start()
        sends.append(copy)

    def across(q, s):
        for n, d in enumerate("RL"):
            go(x_copy(q, xi, d, s, xs_sem.at[q, n, s]))

    def to_ranks(act):
        @pl.loop(1, ranks)
        def _(k):
            peer = (dp + k) % ranks
            act(remote(meta.at[dp], meta.at[dp], ms_sem.at[peer], mr_sem.at[dp], dp=peer))

    start = lambda copy: copy.start()
    wait_send = lambda copy: copy.wait_send()

    def x_stats(buffer, ssem, rsem, k, mine):
        peer = (xi + k) % DP_X
        slot = xi if mine else peer
        return remote(buffer.at[slot], buffer.at[slot], ssem.at[peer], rsem.at[slot], dp=zi * DP_X + peer)

    def z_stats(buffer, ssem, rsem, k, mine):
        peer = (zi + k) % DP_Z
        slot = zi if mine else peer
        return remote(
            buffer.at[slot],
            buffer.at[slot],
            ssem.at[DP_X + peer],
            rsem.at[DP_X + slot],
            dp=peer * DP_X + xi,
        )

    def stats_start(stage, buffer, ssem, rsem):
        for k in range(1, 4):
            go(stage(buffer, ssem, rsem, k, True))

    def stats_sum(stage, buffer, ssem, rsem):
        for k in range(1, 4):
            stage(buffer, ssem, rsem, k, False).wait_recv()
        return (buffer[0] + buffer[1]) + (buffer[2] + buffer[3])

    text_blocks = text_ref.shape[0]

    def project(q):
        plane = planes[q]
        rows = gather[pl.ds(plane * DP_X, DP_X)]
        rows = rows.reshape(DP_X * PIECES * PATCH, rows.shape[-1])
        out = jnp.dot(rows, w_ref[...], preferred_element_type=jnp.float32) + bias_ref[...]
        out = out.astype(jnp.bfloat16)
        images = DP_X * PIECES
        proj[pl.ds(plane * images, images)] = out.reshape(images, PATCH, out.shape[-1])
        for b in range(2):
            pstat_x[xi, plane * 2 + b] = row_sums(out[b * LANES : (b + 1) * LANES])

    def tables():
        @pl.loop(1, ranks)
        def _(k):
            peer = (dp + k) % ranks
            remote(meta.at[peer], meta.at[peer], ms_sem.at[peer], mr_sem.at[peer], dp=peer).wait_recv()

        packed = meta[0]
        for r in range(1, ranks):
            packed = packed + meta[r]
        packed = packed[None]
        owner_row = packed // SPAN
        place_row = packed % SPAN
        shape = (groups, 1, LANES)
        slot = lax.broadcasted_iota(jnp.int32, shape, 2)
        group = lax.broadcasted_iota(jnp.int32, shape, 0)
        named = (owner_row == group) & (slot < ranks * slots)
        first = jnp.min(jnp.where(named, slot, LANES), axis=2, keepdims=True)
        last = jnp.max(jnp.where(named, slot, -1), axis=2, keepdims=True)
        at_first = jnp.max(jnp.where(named & (slot == first), place_row, 0), axis=2, keepdims=True)
        at_last = jnp.max(
            jnp.where(named & (slot == last) & (slot != first), place_row, 0), axis=2, keepdims=True
        )
        first = jnp.minimum(first, ranks * slots - 1)
        last = jnp.maximum(last, 0)
        values = jnp.where(slot == 0, at_first - 1, at_last - 1)
        values = jnp.where(slot == 2, first, values)
        values = jnp.where(slot == 3, last, values)
        table[...] = values
        table_smem.start()
        place_own.start()
        to_groups(table_copy, start)

    def table_copy(peer):
        return remote(table.at[peer], places_ref.at[grp], os_sem.at[peer], or_sem.at[grp], grp=peer)

    def out_copy(peer):
        return remote(outbox.at[peer], arrived_ref.at[grp], as_sem.at[peer], ar_sem.at[grp], grp=peer)

    def to_groups(make, act):
        @pl.loop(1, groups)
        def _(k):
            act(make((grp + k) % groups))

    def text_first():
        loads[7].wait()

        @pl.loop(0, text_blocks)
        def _(b):
            tstat_x[xi, b] = row_sums(text_ref[b])

        stats_start(x_stats, tstat_x, ts_sem, tr_sem)

    def text_second():
        tstat_z[zi] = stats_sum(x_stats, tstat_x, ts_sem, tr_sem)
        stats_start(z_stats, tstat_z, ts_sem, tr_sem)

    def text_third():
        for k in range(1, 4):
            z_stats(tstat_z, ts_sem, tr_sem, k, False).wait_recv()

        @pl.loop(0, text_blocks)
        def _(b):
            total = (tstat_z[0, b] + tstat_z[1, b]) + (tstat_z[2, b] + tstat_z[3, b])
            inverse = lax.rsqrt(total / features + 1e-05)
            rows = text_ref[b].astype(jnp.float32)
            rows = rows * spread(inverse, rows.shape[1]) * ogain_ref[...]
            thid_ref[b] = rows.astype(jnp.bfloat16)

        thid_copy.start()

    thid_copy = pltpu.make_async_copy(thid_ref, thid_hbm, local_sem.at[0])
    table_smem = pltpu.make_async_copy(table, table_s, local_sem.at[1])
    place_own = pltpu.make_async_copy(table.at[grp], places_ref.at[grp], local_sem.at[2])
    out_own = pltpu.make_async_copy(outbox.at[grp], arrived_ref.at[grp], local_sem.at[3])
    work = {"tstat": text_first, "tables": tables, "text2": text_second, "text3": text_third}

    opened = False
    for step in arrival_order():
        if step[0] == "own":
            for d in "UD":
                go(z_copy(d, 1, step[1]))
        elif step[0] == "ownx":
            across(0, step[1])
            if step[1] == PIECES - 1:
                to_ranks(start)
        elif step[0] == "task":
            if step[1] in work:
                work[step[1]]()
            else:
                if not opened:
                    loads[8].wait()
                    opened = True
                project(step[1])
        elif step[0] == "z":
            _, d, age, s = step
            z_arrival(d, age, s).wait_recv()
            if goes_on(d, age, s):
                go(z_copy(d, age + 1, s))
            if age % Z_LO == 0:
                across(plane_of(d, age), s)
        else:
            _, q, d, age, s = step
            source = x_from[d] if age == 1 else x_far
            x_copy(q, source, d, s, xr_sem.at[q, s]).wait_recv()
            if age == 1 and s % 2 == (d == "L"):
                go(x_copy(q, source, d, s, xr_sem.at[q, s]))

    stats_start(x_stats, pstat_x, ps_sem, pr_sem)
    table_smem.wait()
    pstat_z[zi] = stats_sum(x_stats, pstat_x, ps_sem, pr_sem)
    stats_start(z_stats, pstat_z, ps_sem, pr_sem)
    for k in range(1, 4):
        z_stats(pstat_z, ps_sem, pr_sem, k, False).wait_recv()

    @pl.loop(0, pstat_z.shape[1])
    def _(b):
        total = (pstat_z[0, b] + pstat_z[1, b]) + (pstat_z[2, b] + pstat_z[3, b])
        inverse = lax.rsqrt(total / features + 1e-05)
        images = LANES // PATCH
        rows = proj[pl.ds(b * images, images)]
        shape = rows.shape
        rows = rows.reshape(LANES, shape[-1]).astype(jnp.float32)
        rows = rows * spread(inverse, shape[-1]) * ogain_ref[...]
        proj[pl.ds(b * images, images)] = rows.astype(jnp.bfloat16).reshape(shape)

    @pl.loop(0, groups)
    def _(o):
        for r in range(CAP):
            outbox[o, r] = proj[table_s[o, 0, CAP + r]]

    to_groups(out_copy, start)
    out_own.start()

    to_ranks(wait_send)
    to_groups(table_copy, wait_send)
    for copy in sends:
        copy.wait_send()
    thid_copy.wait()
    place_own.wait()

    @pl.loop(1, groups)
    def _(k):
        peer = (grp + k) % groups
        remote(table.at[peer], places_ref.at[peer], os_sem.at[peer], or_sem.at[peer], grp=peer).wait_recv()

    @pl.loop(1, groups)
    def _(k):
        peer = (grp + k) % groups
        remote(outbox.at[peer], arrived_ref.at[peer], as_sem.at[peer], ar_sem.at[peer], grp=peer).wait()

    out_own.wait()


def overlay_kernel(places_ref, thid_ref, arrived_ref, out_ref, rows):
    chunks = rows.shape[0]
    for c in range(chunks):
        rows[c] = thid_ref[:, c * LANES : (c + 1) * LANES].astype(jnp.float32)

    @pl.loop(0, arrived_ref.shape[0])
    def _(g):
        for r in range(CAP):
            at = places_ref[g, 0, r]

            @pl.when(at >= 0)
            def _():
                image = arrived_ref[g, r].astype(jnp.float32)
                for c in range(chunks):
                    rows[c, pl.ds(at, PATCH), :] = image[:, c * LANES : (c + 1) * LANES]

    for c in range(chunks):
        out_ref[:, c * LANES : (c + 1) * LANES] = rows[c].astype(jnp.bfloat16)


def on_device(
    ranks,
    vis_features,
    vis_gain,
    proj_weight,
    proj_bias,
    text_embed,
    out_gain,
    image_counts,
    owner_block,
    offsets,
):
    groups = lax.axis_size("grp")
    width, columns = proj_weight.shape
    seq_len = text_embed.shape[0]
    slots = ranks * owner_block.shape[0]
    text_blocks = seq_len // LANES
    stat_blocks = slots * PATCH // LANES
    bf16, f32, i32 = jnp.bfloat16, jnp.float32, jnp.int32
    vmem = pl.BlockSpec(memory_space=pltpu.VMEM)
    smem = pl.BlockSpec(memory_space=pltpu.SMEM)
    hbm = pl.BlockSpec(memory_space=pltpu.HBM)
    dma = pltpu.SemaphoreType.DMA
    arrived, places, thid = pl.pallas_call(
        functools.partial(exchange_kernel, (groups, ranks, ranks * columns)),
        out_shape=(
            jax.ShapeDtypeStruct((groups, CAP, PATCH, columns), bf16),
            jax.ShapeDtypeStruct((groups, 1, LANES), i32),
            jax.ShapeDtypeStruct((text_blocks, LANES, columns), bf16),
        ),
        in_specs=[hbm] * 9,
        out_specs=(pl.BlockSpec(memory_space=pl.ANY),) * 3,
        scratch_shapes=[
            pltpu.VMEM(vis_features.shape, bf16),
            pltpu.VMEM((width,), f32),
            pltpu.VMEM((columns,), f32),
            pltpu.VMEM((columns,), f32),
            pltpu.SMEM(image_counts.shape, i32),
            pltpu.SMEM(owner_block.shape, i32),
            pltpu.SMEM(offsets.shape, i32),
            pltpu.VMEM((ranks, PIECES, PATCH, width), bf16),
            pltpu.VMEM((2, 2 * Z_LO - 2, PIECES, PATCH, width), bf16),
            pltpu.VMEM((width, columns), bf16),
            pltpu.VMEM((text_blocks, LANES, columns), bf16),
            pltpu.VMEM((text_blocks, LANES, columns), bf16),
            pltpu.VMEM((slots, PATCH, columns), bf16),
            pltpu.VMEM((groups, CAP, PATCH, columns), bf16),
            pltpu.VMEM((ranks, 1, LANES), i32),
            pltpu.VMEM((groups, 1, LANES), i32),
            pltpu.SMEM((groups, 1, LANES), i32),
            pltpu.VMEM((DP_X, text_blocks, 1, LANES), f32),
            pltpu.VMEM((DP_Z, text_blocks, 1, LANES), f32),
            pltpu.VMEM((DP_X, stat_blocks, 1, LANES), f32),
            pltpu.VMEM((DP_Z, stat_blocks, 1, LANES), f32),
            dma((13,)),
            dma((2, 2 * Z_LO, PIECES)),
            dma((2, 2 * Z_LO, PIECES)),
            dma((DP_Z, 2, PIECES)),
            dma((DP_Z, PIECES)),
            dma((ranks, PIECES)),
            dma((ranks,)),
            dma((ranks,)),
            dma((DP_X + DP_Z,)),
            dma((DP_X + DP_Z,)),
            dma((DP_X + DP_Z,)),
            dma((DP_X + DP_Z,)),
            dma((groups,)),
            dma((groups,)),
            dma((groups,)),
            dma((groups,)),
        ],
        compiler_params=pltpu.CompilerParams(
            collective_id=0, has_side_effects=True, vmem_limit_bytes=48 << 20
        ),
        name="exchange",
    )(
        vis_features,
        vis_gain,
        proj_weight,
        proj_bias,
        text_embed.reshape(text_blocks, LANES, columns),
        out_gain,
        image_counts,
        owner_block,
        offsets,
    )
    return pl.pallas_call(
        overlay_kernel,
        out_shape=jax.ShapeDtypeStruct((seq_len, columns), bf16),
        in_specs=[smem, vmem, vmem],
        out_specs=vmem,
        scratch_shapes=[pltpu.VMEM((columns // LANES, seq_len, LANES), f32)],
        compiler_params=pltpu.CompilerParams(vmem_limit_bytes=32 << 20),
        name="overlay",
    )(places, thid.reshape(seq_len, columns), arrived)


def solution(mesh):
    return jax.shard_map(
        functools.partial(on_device, mesh.shape["dp"]),
        mesh=mesh,
        in_specs=(
            P(("grp", "dp"), None),
            P(),
            P(None, "dp"),
            P("dp"),
            P("grp", "dp"),
            P("dp"),
            P(("grp", "dp")),
            P(("grp", "dp")),
            P(("grp", "dp")),
        ),
        out_specs=P("grp", "dp"),
        check_vma=False,
    )
```

```python
import functools

import jax
import jax.numpy as jnp
from jax import lax
from jax.experimental import pallas as pl
from jax.experimental.pallas import tpu as pltpu
from jax.sharding import PartitionSpec as P

MESH = pl.DeviceIdType.MESH
PATCH = 16
CAP = 2
DP_X = 4
DP_Z = 4
PIECES = 4
Z_LO = 3
CORES = 2
SPAN = 2048
LANES = 128


def row_sums(values):
    f = values.astype(jnp.float32)
    sq = f * f
    part = sq[:, :LANES]
    for c in range(1, values.shape[1] // LANES):
        part = part + sq[:, c * LANES : (c + 1) * LANES]
    return jnp.sum(part.T, axis=0, keepdims=True)


def spread(row, columns):
    square = jnp.broadcast_to(row, (LANES, LANES)).T
    return jnp.concatenate([square] * (columns // LANES), axis=1)


def arrival_order(piece=1.1, latency=1.6, ahead=4):
    free = dict.fromkeys("UDRL", 0.0)
    now = 0.0
    pending = {}
    order = []

    def send(link, key):
        free[link] = max(free[link], now) + piece
        pending[key] = free[link] + latency

    def own(s):
        order.append(("own", s))
        for d in "UD":
            send(d, ("z", d, 1, s))

    def across(q, s):
        for d in "RL":
            send(d, ("x", q, d, 1, s))

    for s in range(PIECES):
        if s < ahead:
            own(s)
        order.append(("ownx", s))
        across(0, s)
    following = ahead
    count = [0] * DP_Z
    tasks = []
    while pending or tasks:
        here = [k for k, t in pending.items() if t <= now]
        ready = [t for t in tasks if t[0] <= now]
        if not here and ready:
            tasks.remove(ready[0])
            order.append(("task", ready[0][1]))
            now += ready[0][2]
            continue
        if not here:
            now = min([*pending.values(), *[t[0] for t in tasks]])
            continue
        key = min(here, key=lambda k: pending[k])
        del pending[key]
        order.append(key)
        now += 0.06
        if key[0] == "z":
            _, d, age, s = key
            if goes_on(d, age, s):
                send(d, ("z", d, age + 1, s))
            if age % Z_LO == 0:
                across(plane_of(d, age), s)
            if age == 1 and d == "D" and following < PIECES:
                own(following)
                following += 1
        else:
            _, q, d, age, s = key
            if age == 1 and s % 2 == (d == "L"):
                send(d, ("x", q, d, 2, s))
            count[q] += 1
            if count[q] == (DP_X - 1) * PIECES:
                tasks.append((now, q, 3.0))
    return order


def goes_on(d, age, s):
    return age < Z_LO or (age < 2 * Z_LO and s % 2 == (d == "D"))


def plane_of(d, age):
    return 3 if age == 2 * Z_LO else 1 if d == "U" else 2


def exchange_kernel(
    dims,
    vis_hbm,
    vgain_hbm,
    w_hbm,
    bias_hbm,
    text_hbm,
    ogain_hbm,
    count_hbm,
    owner_hbm,
    offset_hbm,
    arrived_ref,
    places_ref,
    thid_hbm,
    vis_ref,
    vgain_ref,
    bias_ref,
    ogain_ref,
    count_ref,
    owner_ref,
    offset_ref,
    gather,
    passing,
    w_ref,
    text_ref,
    thid_ref,
    proj,
    outbox,
    meta,
    table,
    table_s,
    tstat_x,
    tstat_z,
    pstat_x,
    pstat_z,
    local_sem,
    zs_sem,
    zg_sem,
    xs_sem,
    xr_sem,
    g_sem,
    ms_sem,
    mr_sem,
    ts_sem,
    tr_sem,
    ps_sem,
    pr_sem,
    os_sem,
    or_sem,
    as_sem,
    ar_sem,
    turn_sem,
):
    groups, ranks, features = dims
    grp = lax.axis_index("grp")
    dp = lax.axis_index("dp")
    zi, xi = dp // DP_X, dp % DP_X
    core, z_lo, y = grp % CORES, grp // CORES % Z_LO, grp // CORES // Z_LO
    z = zi * Z_LO + z_lo
    z_ring = DP_Z * Z_LO
    planes = (zi, (zi + 3) % DP_Z, (zi + 1) % DP_Z, (zi + 2) % DP_Z)
    x_next = {"R": (xi + 1) % DP_X, "L": (xi + 3) % DP_X}
    x_from = {"R": (xi + 3) % DP_X, "L": (xi + 1) % DP_X}
    x_far = (xi + 2) % DP_X

    def z_device(at):
        return {"grp": (y * Z_LO + at % Z_LO) * CORES + core, "dp": at // Z_LO * DP_X + xi}

    z_next = {"U": z_device((z + 1) % z_ring), "D": z_device((z + z_ring - 1) % z_ring)}

    def remote(src, dst, ssem, rsem, **where):
        return pltpu.make_async_remote_copy(
            src_ref=src, dst_ref=dst, send_sem=ssem, recv_sem=rsem, device_id=where, device_id_type=MESH
        )

    loads = [
        pltpu.make_async_copy(src, dst, local_sem.at[4 + n])
        for n, (src, dst) in enumerate(
            [
                (vis_hbm, vis_ref),
                (vgain_hbm, vgain_ref),
                (owner_hbm, owner_ref),
                (offset_hbm, offset_ref),
                (count_hbm, count_ref),
                (bias_hbm, bias_ref),
                (ogain_hbm, ogain_ref),
                (text_hbm, text_ref),
                (w_hbm, w_ref),
            ]
        )
    ]
    for copy in loads:
        copy.start()

    barrier = pltpu.get_barrier_semaphore()

    for d in "UD":
        pl.semaphore_signal(barrier, inc=1, device_id=z_next[d], device_id_type=MESH)

    @pl.loop(1, ranks)
    def _(k):
        pl.semaphore_signal(barrier, inc=1, device_id={"dp": (dp + k) % ranks}, device_id_type=MESH)

    @pl.loop(1, groups)
    def _(k):
        pl.semaphore_signal(barrier, inc=1, device_id={"grp": (grp + k) % groups}, device_id_type=MESH)

    for copy in loads[:7]:
        copy.wait()
    f = vis_ref[...].astype(jnp.float32)
    normed = (
        f * lax.rsqrt(jnp.mean(f * f, axis=-1, keepdims=True) + 1e-06) * vgain_ref[...]
    ).astype(jnp.bfloat16)
    gather[dp] = normed.reshape(gather.shape[1:])

    lane = lax.broadcasted_iota(jnp.int32, (1, LANES), 1)
    packed = jnp.zeros((1, LANES), jnp.int32)
    slots = owner_ref.shape[0]
    for j in range(slots):
        live = jnp.full((1, LANES), count_ref[0], jnp.int32) > j
        value = owner_ref[j] * SPAN + jnp.where(live, offset_ref[j] + 1, 0)
        packed = jnp.where(lane == dp * slots + j, value, packed)
    meta[dp] = packed

    pl.semaphore_wait(barrier, ranks - 1 + groups - 1 + 2)

    def z_source(d, age):
        return ((z + z_ring - age if d == "U" else z + age) % z_ring) // Z_LO

    def z_slot(d, age, s, arriving):
        if age % Z_LO == 0:
            return gather.at[z_source(d, age) * DP_X + xi, s]
        return passing.at["UD".index(d), age - 1 - age // Z_LO, s]

    def z_copy(d, age, s):
        if age % Z_LO == 0:
            target = gather.at[z_source(d, age - 1) * DP_X + xi, s]
        else:
            target = passing.at["UD".index(d), age - 1 - age // Z_LO, s]
        n = "UD".index(d)
        return remote(
            z_slot(d, age - 1, s, False), target, zs_sem.at[n, age - 1, s], zg_sem.at[n, age - 1, s], **z_next[d]
        )

    def z_arrival(d, age, s):
        n = "UD".index(d)
        piece = z_slot(d, age, s, True)
        return remote(piece, piece, zs_sem.at[n, age - 1, s], zg_sem.at[n, age - 1, s], **z_next[d])

    def x_copy(q, source, d, s, sem):
        place = planes[q] * DP_X + source
        piece = gather.at[place, s]
        return remote(piece, piece, sem, g_sem.at[place, s], dp=zi * DP_X + x_next[d])

    sends = []

    def go(copy):
        copy.start()
        sends.append(copy)

    def across(q, s):
        for n, d in enumerate("RL"):
            go(x_copy(q, xi, d, s, xs_sem.at[q, n, s]))

    def to_ranks(act):
        @pl.loop(1, ranks)
        def _(k):
            peer = (dp + k) % ranks
            act(remote(meta.at[dp], meta.at[dp], ms_sem.at[peer], mr_sem.at[dp], dp=peer))

    start = lambda copy: copy.start()
    wait_send = lambda copy: copy.wait_send()

    def x_stats(buffer, ssem, rsem, k, mine):
        peer = (xi + k) % DP_X
        slot = xi if mine else peer
        return remote(buffer.at[slot], buffer.at[slot], ssem.at[peer], rsem.at[slot], dp=zi * DP_X + peer)

    def z_stats(buffer, ssem, rsem, k, mine):
        peer = (zi + k) % DP_Z
        slot = zi if mine else peer
        return remote(
            buffer.at[slot],
            buffer.at[slot],
            ssem.at[DP_X + peer],
            rsem.at[DP_X + slot],
            dp=peer * DP_X + xi,
        )

    def stats_start(stage, buffer, ssem, rsem):
        for k in range(1, 4):
            go(stage(buffer, ssem, rsem, k, True))

    def stats_sum(stage, buffer, ssem, rsem):
        for k in range(1, 4):
            stage(buffer, ssem, rsem, k, False).wait_recv()
        return (buffer[0] + buffer[1]) + (buffer[2] + buffer[3])

    text_blocks = text_ref.shape[0]

    def project(q):
        plane = planes[q]
        rows = gather[pl.ds(plane * DP_X, DP_X)]
        rows = rows.reshape(DP_X * PIECES * PATCH, rows.shape[-1])
        out = jnp.dot(rows, w_ref[...], preferred_element_type=jnp.float32) + bias_ref[...]
        out = out.astype(jnp.bfloat16)
        images = DP_X * PIECES
        proj[pl.ds(plane * images, images)] = out.reshape(images, PATCH, out.shape[-1])
        for b in range(2):
            pstat_x[xi, plane * 2 + b] = row_sums(out[b * LANES : (b + 1) * LANES])

    def tables():
        @pl.loop(1, ranks)
        def _(k):
            peer = (dp + k) % ranks
            remote(meta.at[peer], meta.at[peer], ms_sem.at[peer], mr_sem.at[peer], dp=peer).wait_recv()

        packed = meta[0]
        for r in range(1, ranks):
            packed = packed + meta[r]
        packed = packed[None]
        owner_row = packed // SPAN
        place_row = packed % SPAN
        shape = (groups, 1, LANES)
        slot = lax.broadcasted_iota(jnp.int32, shape, 2)
        group = lax.broadcasted_iota(jnp.int32, shape, 0)
        named = (owner_row == group) & (slot < ranks * slots)
        first = jnp.min(jnp.where(named, slot, LANES), axis=2, keepdims=True)
        last = jnp.max(jnp.where(named, slot, -1), axis=2, keepdims=True)
        at_first = jnp.max(jnp.where(named & (slot == first), place_row, 0), axis=2, keepdims=True)
        at_last = jnp.max(
            jnp.where(named & (slot == last) & (slot != first), place_row, 0), axis=2, keepdims=True
        )
        first = jnp.minimum(first, ranks * slots - 1)
        last = jnp.maximum(last, 0)
        values = jnp.where(slot == 0, at_first - 1, at_last - 1)
        values = jnp.where(slot == 2, first, values)
        values = jnp.where(slot == 3, last, values)
        table[...] = values
        table_smem.start()

    def table_copy(peer):
        return remote(table.at[peer], places_ref.at[grp], os_sem.at[peer], or_sem.at[grp], grp=peer)

    def out_copy(peer):
        return remote(outbox.at[peer], arrived_ref.at[grp], as_sem.at[peer], ar_sem.at[grp], grp=peer)

    def to_groups(make, act):
        @pl.loop(1, groups)
        def _(k):
            act(make((grp + k) % groups))

    def text_first():
        loads[7].wait()

        @pl.loop(0, text_blocks)
        def _(b):
            tstat_x[xi, b] = row_sums(text_ref[b])

        stats_start(x_stats, tstat_x, ts_sem, tr_sem)

    def text_second():
        tstat_z[zi] = stats_sum(x_stats, tstat_x, ts_sem, tr_sem)
        stats_start(z_stats, tstat_z, ts_sem, tr_sem)

    def text_third():
        for k in range(1, 4):
            z_stats(tstat_z, ts_sem, tr_sem, k, False).wait_recv()

        @pl.loop(0, text_blocks)
        def _(b):
            total = (tstat_z[0, b] + tstat_z[1, b]) + (tstat_z[2, b] + tstat_z[3, b])
            inverse = lax.rsqrt(total / features + 1e-05)
            rows = text_ref[b].astype(jnp.float32)
            rows = rows * spread(inverse, rows.shape[1]) * ogain_ref[...]
            thid_ref[b] = rows.astype(jnp.bfloat16)

        thid_copy.start()

    thid_copy = pltpu.make_async_copy(thid_ref, thid_hbm, local_sem.at[0])
    table_smem = pltpu.make_async_copy(table, table_s, local_sem.at[1])
    place_own = pltpu.make_async_copy(table.at[grp], places_ref.at[grp], local_sem.at[2])
    out_own = pltpu.make_async_copy(outbox.at[grp], arrived_ref.at[grp], local_sem.at[3])

    @pl.when(core == 1)
    def _():
        pl.semaphore_wait(turn_sem, 1)

    opened = False
    order = arrival_order()
    handover = 1 + max(n for n, step in enumerate(order) if step[0] == "z" and step[2] <= 1)
    for n, step in enumerate(order):
        if n == handover:

            @pl.when(core == 0)
            def _():
                pl.semaphore_signal(turn_sem, inc=1, device_id={"grp": grp + 1 - 2 * core}, device_id_type=MESH)

        if step[0] == "own":
            for d in "UD":
                go(z_copy(d, 1, step[1]))
        elif step[0] == "ownx":
            across(0, step[1])
            if step[1] == PIECES - 1:
                to_ranks(start)
        elif step[0] == "task":
            if not opened:
                loads[8].wait()
                opened = True
            project(step[1])
        elif step[0] == "z":
            _, d, age, s = step
            z_arrival(d, age, s).wait_recv()
            if goes_on(d, age, s):
                go(z_copy(d, age + 1, s))
            if age % Z_LO == 0:
                across(plane_of(d, age), s)
        else:
            _, q, d, age, s = step
            source = x_from[d] if age == 1 else x_far
            x_copy(q, source, d, s, xr_sem.at[q, s]).wait_recv()
            if age == 1 and s % 2 == (d == "L"):
                go(x_copy(q, source, d, s, xr_sem.at[q, s]))

    stats_start(x_stats, pstat_x, ps_sem, pr_sem)
    tables()
    pstat_z[zi] = stats_sum(x_stats, pstat_x, ps_sem, pr_sem)
    stats_start(z_stats, pstat_z, ps_sem, pr_sem)
    table_smem.wait()
    for k in range(1, 4):
        z_stats(pstat_z, ps_sem, pr_sem, k, False).wait_recv()

    @pl.loop(0, pstat_z.shape[1])
    def _(b):
        total = (pstat_z[0, b] + pstat_z[1, b]) + (pstat_z[2, b] + pstat_z[3, b])
        inverse = lax.rsqrt(total / features + 1e-05)
        images = LANES // PATCH
        rows = proj[pl.ds(b * images, images)]
        shape = rows.shape
        rows = rows.reshape(LANES, shape[-1]).astype(jnp.float32)
        rows = rows * spread(inverse, shape[-1]) * ogain_ref[...]
        proj[pl.ds(b * images, images)] = rows.astype(jnp.bfloat16).reshape(shape)

    @pl.loop(0, groups)
    def _(o):
        for r in range(CAP):
            outbox[o, r] = proj[table_s[o, 0, CAP + r]]

    to_groups(out_copy, start)
    out_own.start()
    place_own.start()
    to_groups(table_copy, start)

    text_first()
    text_second()
    text_third()

    to_ranks(wait_send)
    to_groups(table_copy, wait_send)
    for copy in sends:
        copy.wait_send()
    thid_copy.wait()
    place_own.wait()

    @pl.loop(1, groups)
    def _(k):
        peer = (grp + k) % groups
        remote(table.at[peer], places_ref.at[peer], os_sem.at[peer], or_sem.at[peer], grp=peer).wait_recv()

    @pl.loop(1, groups)
    def _(k):
        peer = (grp + k) % groups
        remote(outbox.at[peer], arrived_ref.at[peer], as_sem.at[peer], ar_sem.at[peer], grp=peer).wait()

    out_own.wait()


def overlay_kernel(places_hbm, thid_hbm, arrived_hbm, out_hbm, places_ref, thid_ref, arrived_ref, rows, sem):
    chunks = rows.shape[0]
    blocks = thid_ref.shape[0]
    places_copy = pltpu.make_async_copy(places_hbm, places_ref, sem.at[0])
    arrived_copy = pltpu.make_async_copy(arrived_hbm, arrived_ref, sem.at[1])
    loads = [pltpu.make_async_copy(thid_hbm.at[b], thid_ref.at[b], sem.at[2 + b]) for b in range(blocks)]
    for copy in [places_copy, *loads, arrived_copy]:
        copy.start()
    for b in range(blocks):
        loads[b].wait()
        for c in range(chunks):
            rows[c, b * LANES : (b + 1) * LANES] = thid_ref[b, :, c * LANES : (c + 1) * LANES].astype(jnp.float32)
    places_copy.wait()
    arrived_copy.wait()

    @pl.loop(0, arrived_ref.shape[0])
    def _(g):
        for r in range(CAP):
            at = places_ref[g, 0, r]

            @pl.when(at >= 0)
            def _():
                image = arrived_ref[g, r].astype(jnp.float32)
                for c in range(chunks):
                    rows[c, pl.ds(at, PATCH), :] = image[:, c * LANES : (c + 1) * LANES]

    stores = []
    for b in range(blocks):
        for c in range(chunks):
            thid_ref[b, :, c * LANES : (c + 1) * LANES] = rows[c, b * LANES : (b + 1) * LANES].astype(jnp.bfloat16)
        copy = pltpu.make_async_copy(thid_ref.at[b], out_hbm.at[b], sem.at[2 + b])
        copy.start()
        stores.append(copy)
    for copy in stores:
        copy.wait()


def on_device(
    ranks,
    vis_features,
    vis_gain,
    proj_weight,
    proj_bias,
    text_embed,
    out_gain,
    image_counts,
    owner_block,
    offsets,
):
    groups = lax.axis_size("grp")
    width, columns = proj_weight.shape
    seq_len = text_embed.shape[0]
    slots = ranks * owner_block.shape[0]
    text_blocks = seq_len // LANES
    stat_blocks = slots * PATCH // LANES
    bf16, f32, i32 = jnp.bfloat16, jnp.float32, jnp.int32
    hbm = pl.BlockSpec(memory_space=pltpu.HBM)
    dma = pltpu.SemaphoreType.DMA
    arrived, places, thid = pl.pallas_call(
        functools.partial(exchange_kernel, (groups, ranks, ranks * columns)),
        out_shape=(
            jax.ShapeDtypeStruct((groups, CAP, PATCH, columns), bf16),
            jax.ShapeDtypeStruct((groups, 1, LANES), i32),
            jax.ShapeDtypeStruct((text_blocks, LANES, columns), bf16),
        ),
        in_specs=[hbm] * 9,
        out_specs=(pl.BlockSpec(memory_space=pl.ANY),) * 3,
        scratch_shapes=[
            pltpu.VMEM(vis_features.shape, bf16),
            pltpu.VMEM((width,), f32),
            pltpu.VMEM((columns,), f32),
            pltpu.VMEM((columns,), f32),
            pltpu.SMEM(image_counts.shape, i32),
            pltpu.SMEM(owner_block.shape, i32),
            pltpu.SMEM(offsets.shape, i32),
            pltpu.VMEM((ranks, PIECES, PATCH, width), bf16),
            pltpu.VMEM((2, 2 * Z_LO - 2, PIECES, PATCH, width), bf16),
            pltpu.VMEM((width, columns), bf16),
            pltpu.VMEM((text_blocks, LANES, columns), bf16),
            pltpu.VMEM((text_blocks, LANES, columns), bf16),
            pltpu.VMEM((slots, PATCH, columns), bf16),
            pltpu.VMEM((groups, CAP, PATCH, columns), bf16),
            pltpu.VMEM((ranks, 1, LANES), i32),
            pltpu.VMEM((groups, 1, LANES), i32),
            pltpu.SMEM((groups, 1, LANES), i32),
            pltpu.VMEM((DP_X, text_blocks, 1, LANES), f32),
            pltpu.VMEM((DP_Z, text_blocks, 1, LANES), f32),
            pltpu.VMEM((DP_X, stat_blocks, 1, LANES), f32),
            pltpu.VMEM((DP_Z, stat_blocks, 1, LANES), f32),
            dma((13,)),
            dma((2, 2 * Z_LO, PIECES)),
            dma((2, 2 * Z_LO, PIECES)),
            dma((DP_Z, 2, PIECES)),
            dma((DP_Z, PIECES)),
            dma((ranks, PIECES)),
            dma((ranks,)),
            dma((ranks,)),
            dma((DP_X + DP_Z,)),
            dma((DP_X + DP_Z,)),
            dma((DP_X + DP_Z,)),
            dma((DP_X + DP_Z,)),
            dma((groups,)),
            dma((groups,)),
            dma((groups,)),
            dma((groups,)),
            pltpu.SemaphoreType.REGULAR,
        ],
        compiler_params=pltpu.CompilerParams(
            collective_id=0, has_side_effects=True, vmem_limit_bytes=60 << 20
        ),
        name="exchange",
    )(
        vis_features,
        vis_gain,
        proj_weight,
        proj_bias,
        text_embed.reshape(text_blocks, LANES, columns),
        out_gain,
        image_counts,
        owner_block,
        offsets,
    )
    hidden = pl.pallas_call(
        overlay_kernel,
        out_shape=jax.ShapeDtypeStruct((text_blocks, LANES, columns), bf16),
        in_specs=[hbm] * 3,
        out_specs=pl.BlockSpec(memory_space=pl.ANY),
        scratch_shapes=[
            pltpu.SMEM((groups, 1, LANES), i32),
            pltpu.VMEM((text_blocks, LANES, columns), bf16),
            pltpu.VMEM((groups, CAP, PATCH, columns), bf16),
            pltpu.VMEM((columns // LANES, seq_len, LANES), f32),
            dma((2 + text_blocks,)),
        ],
        compiler_params=pltpu.CompilerParams(vmem_limit_bytes=60 << 20),
        name="overlay",
    )(places, thid, arrived)
    return hidden.reshape(seq_len, columns)


def solution(mesh):
    return jax.shard_map(
        functools.partial(on_device, mesh.shape["dp"]),
        mesh=mesh,
        in_specs=(
            P(("grp", "dp"), None),
            P(),
            P(None, "dp"),
            P("dp"),
            P("grp", "dp"),
            P("dp"),
            P(("grp", "dp")),
            P(("grp", "dp")),
            P(("grp", "dp")),
        ),
        out_specs=P("grp", "dp"),
        check_vma=False,
    )
```

```python
import functools

import jax
import jax.numpy as jnp
from jax import lax
from jax.experimental import pallas as pl
from jax.experimental.pallas import tpu as pltpu
from jax.sharding import PartitionSpec as P

MESH = pl.DeviceIdType.MESH
PATCH = 16
CAP = 2
DP_X = 4
DP_Z = 4
PIECES = 4
Z_LO = 3
CORES = 2
SPAN = 2048
LANES = 128


def row_sums(values):
    f = values.astype(jnp.float32)
    sq = f * f
    part = sq[:, :LANES]
    for c in range(1, values.shape[1] // LANES):
        part = part + sq[:, c * LANES : (c + 1) * LANES]
    return jnp.sum(part.T, axis=0, keepdims=True)


def spread(row, columns):
    square = jnp.broadcast_to(row, (LANES, LANES)).T
    return jnp.concatenate([square] * (columns // LANES), axis=1)


def arrival_order(piece=1.1, latency=1.6, ahead=4):
    free = dict.fromkeys("UDRL", 0.0)
    now = 0.0
    pending = {}
    order = []

    def send(link, key):
        free[link] = max(free[link], now) + piece
        pending[key] = free[link] + latency

    def own(s):
        order.append(("own", s))
        for d in "UD":
            send(d, ("z", d, 1, s))

    def across(q, s):
        for d in "RL":
            send(d, ("x", q, d, 1, s))

    for s in range(PIECES):
        if s < ahead:
            own(s)
        order.append(("ownx", s))
        across(0, s)
    following = ahead
    count = [0] * DP_Z
    tasks = []
    while pending or tasks:
        here = [k for k, t in pending.items() if t <= now]
        ready = [t for t in tasks if t[0] <= now]
        if not here and ready:
            tasks.remove(ready[0])
            order.append(("task", ready[0][1]))
            now += ready[0][2]
            continue
        if not here:
            now = min([*pending.values(), *[t[0] for t in tasks]])
            continue
        key = min(here, key=lambda k: pending[k])
        del pending[key]
        order.append(key)
        now += 0.06
        if key[0] == "z":
            _, d, age, s = key
            if goes_on(d, age, s):
                send(d, ("z", d, age + 1, s))
            if age % Z_LO == 0:
                across(plane_of(d, age), s)
            if age == 1 and d == "D" and following < PIECES:
                own(following)
                following += 1
        else:
            _, q, d, age, s = key
            if age == 1 and s % 2 == (d == "L"):
                send(d, ("x", q, d, 2, s))
            count[q] += 1
            if count[q] == (DP_X - 1) * PIECES:
                tasks.append((now, q, 3.0))
    return order


def goes_on(d, age, s):
    return age < Z_LO or (age < 2 * Z_LO and s % 2 == (d == "D"))


def plane_of(d, age):
    return 3 if age == 2 * Z_LO else 1 if d == "U" else 2


def exchange_kernel(
    dims,
    vis_hbm,
    vgain_hbm,
    w_hbm,
    bias_hbm,
    text_hbm,
    ogain_hbm,
    count_hbm,
    owner_hbm,
    offset_hbm,
    arrived_ref,
    places_ref,
    thid_hbm,
    vis_ref,
    vgain_ref,
    bias_ref,
    ogain_ref,
    count_ref,
    owner_ref,
    offset_ref,
    gather,
    passing,
    w_ref,
    text_ref,
    thid_ref,
    proj,
    outbox,
    meta,
    table,
    table_s,
    tstat_x,
    tstat_z,
    pstat_x,
    pstat_z,
    local_sem,
    zs_sem,
    zg_sem,
    xs_sem,
    xr_sem,
    g_sem,
    ms_sem,
    mr_sem,
    ts_sem,
    tr_sem,
    ps_sem,
    pr_sem,
    os_sem,
    or_sem,
    as_sem,
    ar_sem,
    turn_sem,
):
    groups, ranks, features = dims
    grp = lax.axis_index("grp")
    dp = lax.axis_index("dp")
    zi, xi = dp // DP_X, dp % DP_X
    core, z_lo, y = grp % CORES, grp // CORES % Z_LO, grp // CORES // Z_LO
    z = zi * Z_LO + z_lo
    z_ring = DP_Z * Z_LO
    planes = (zi, (zi + 3) % DP_Z, (zi + 1) % DP_Z, (zi + 2) % DP_Z)
    x_next = {"R": (xi + 1) % DP_X, "L": (xi + 3) % DP_X}
    x_from = {"R": (xi + 3) % DP_X, "L": (xi + 1) % DP_X}
    x_far = (xi + 2) % DP_X

    def z_device(at):
        return {"grp": (y * Z_LO + at % Z_LO) * CORES + core, "dp": at // Z_LO * DP_X + xi}

    z_next = {"U": z_device((z + 1) % z_ring), "D": z_device((z + z_ring - 1) % z_ring)}

    def remote(src, dst, ssem, rsem, **where):
        return pltpu.make_async_remote_copy(
            src_ref=src, dst_ref=dst, send_sem=ssem, recv_sem=rsem, device_id=where, device_id_type=MESH
        )

    loads = [
        pltpu.make_async_copy(src, dst, local_sem.at[4 + n])
        for n, (src, dst) in enumerate(
            [
                (vis_hbm, vis_ref),
                (vgain_hbm, vgain_ref),
                (owner_hbm, owner_ref),
                (offset_hbm, offset_ref),
                (count_hbm, count_ref),
                (bias_hbm, bias_ref),
                (ogain_hbm, ogain_ref),
                (text_hbm, text_ref),
                (w_hbm, w_ref),
            ]
        )
    ]
    for copy in loads:
        copy.start()

    barrier = pltpu.get_barrier_semaphore()

    for d in "UD":
        pl.semaphore_signal(barrier, inc=1, device_id=z_next[d], device_id_type=MESH)

    @pl.loop(1, ranks)
    def _(k):
        pl.semaphore_signal(barrier, inc=1, device_id={"dp": (dp + k) % ranks}, device_id_type=MESH)

    @pl.loop(1, groups)
    def _(k):
        pl.semaphore_signal(barrier, inc=1, device_id={"grp": (grp + k) % groups}, device_id_type=MESH)

    for copy in loads[:7]:
        copy.wait()
    f = vis_ref[...].astype(jnp.float32)
    normed = (
        f * lax.rsqrt(jnp.mean(f * f, axis=-1, keepdims=True) + 1e-06) * vgain_ref[...]
    ).astype(jnp.bfloat16)
    gather[dp] = normed.reshape(gather.shape[1:])

    lane = lax.broadcasted_iota(jnp.int32, (1, LANES), 1)
    packed = jnp.zeros((1, LANES), jnp.int32)
    slots = owner_ref.shape[0]
    for j in range(slots):
        live = jnp.full((1, LANES), count_ref[0], jnp.int32) > j
        value = owner_ref[j] * SPAN + jnp.where(live, offset_ref[j] + 1, 0)
        packed = jnp.where(lane == dp * slots + j, value, packed)
    meta[dp] = packed

    pl.semaphore_wait(barrier, ranks - 1 + groups - 1 + 2)

    def z_source(d, age):
        return ((z + z_ring - age if d == "U" else z + age) % z_ring) // Z_LO

    def z_slot(d, age, s, arriving):
        if age % Z_LO == 0:
            return gather.at[z_source(d, age) * DP_X + xi, s]
        return passing.at["UD".index(d), age - 1 - age // Z_LO, s]

    def z_copy(d, age, s):
        if age % Z_LO == 0:
            target = gather.at[z_source(d, age - 1) * DP_X + xi, s]
        else:
            target = passing.at["UD".index(d), age - 1 - age // Z_LO, s]
        n = "UD".index(d)
        return remote(
            z_slot(d, age - 1, s, False), target, zs_sem.at[n, age - 1, s], zg_sem.at[n, age - 1, s], **z_next[d]
        )

    def z_arrival(d, age, s):
        n = "UD".index(d)
        piece = z_slot(d, age, s, True)
        return remote(piece, piece, zs_sem.at[n, age - 1, s], zg_sem.at[n, age - 1, s], **z_next[d])

    def x_copy(q, source, d, s, sem):
        place = planes[q] * DP_X + source
        piece = gather.at[place, s]
        return remote(piece, piece, sem, g_sem.at[place, s], dp=zi * DP_X + x_next[d])

    sends = []

    def go(copy):
        copy.start()
        sends.append(copy)

    def across(q, s):
        for n, d in enumerate("RL"):
            go(x_copy(q, xi, d, s, xs_sem.at[q, n, s]))

    def to_ranks(act):
        @pl.loop(1, ranks)
        def _(k):
            peer = (dp + k) % ranks
            act(remote(meta.at[dp], meta.at[dp], ms_sem.at[peer], mr_sem.at[dp], dp=peer))

    start = lambda copy: copy.start()
    wait_send = lambda copy: copy.wait_send()

    def x_stats(buffer, ssem, rsem, k, mine):
        peer = (xi + k) % DP_X
        slot = xi if mine else peer
        return remote(buffer.at[slot], buffer.at[slot], ssem.at[peer], rsem.at[slot], dp=zi * DP_X + peer)

    def z_stats(buffer, ssem, rsem, k, mine):
        peer = (zi + k) % DP_Z
        slot = zi if mine else peer
        return remote(
            buffer.at[slot],
            buffer.at[slot],
            ssem.at[DP_X + peer],
            rsem.at[DP_X + slot],
            dp=peer * DP_X + xi,
        )

    def stats_start(stage, buffer, ssem, rsem):
        for k in range(1, 4):
            go(stage(buffer, ssem, rsem, k, True))

    def stats_sum(stage, buffer, ssem, rsem):
        for k in range(1, 4):
            stage(buffer, ssem, rsem, k, False).wait_recv()
        return (buffer[0] + buffer[1]) + (buffer[2] + buffer[3])

    text_blocks = text_ref.shape[0]

    def project(q):
        plane = planes[q]
        rows = gather[pl.ds(plane * DP_X, DP_X)]
        rows = rows.reshape(DP_X * PIECES * PATCH, rows.shape[-1])
        out = jnp.dot(rows, w_ref[...], preferred_element_type=jnp.float32) + bias_ref[...]
        out = out.astype(jnp.bfloat16)
        images = DP_X * PIECES
        proj[pl.ds(plane * images, images)] = out.reshape(images, PATCH, out.shape[-1])
        for b in range(2):
            pstat_x[xi, plane * 2 + b] = row_sums(out[b * LANES : (b + 1) * LANES])

    def tables():
        @pl.loop(1, ranks)
        def _(k):
            peer = (dp + k) % ranks
            remote(meta.at[peer], meta.at[peer], ms_sem.at[peer], mr_sem.at[peer], dp=peer).wait_recv()

        packed = meta[0]
        for r in range(1, ranks):
            packed = packed + meta[r]
        packed = packed[None]
        owner_row = packed // SPAN
        place_row = packed % SPAN
        shape = (groups, 1, LANES)
        slot = lax.broadcasted_iota(jnp.int32, shape, 2)
        group = lax.broadcasted_iota(jnp.int32, shape, 0)
        named = (owner_row == group) & (slot < ranks * slots)
        first = jnp.min(jnp.where(named, slot, LANES), axis=2, keepdims=True)
        last = jnp.max(jnp.where(named, slot, -1), axis=2, keepdims=True)
        at_first = jnp.max(jnp.where(named & (slot == first), place_row, 0), axis=2, keepdims=True)
        at_last = jnp.max(
            jnp.where(named & (slot == last) & (slot != first), place_row, 0), axis=2, keepdims=True
        )
        first = jnp.minimum(first, ranks * slots - 1)
        last = jnp.maximum(last, 0)
        values = jnp.where(slot == 0, at_first - 1, at_last - 1)
        values = jnp.where(slot == 2, first, values)
        values = jnp.where(slot == 3, last, values)
        table[...] = values
        table_smem.start()

    def table_copy(peer):
        return remote(table.at[peer], places_ref.at[grp], os_sem.at[peer], or_sem.at[grp], grp=peer)

    def out_copy(peer):
        return remote(outbox.at[peer], arrived_ref.at[grp], as_sem.at[peer], ar_sem.at[grp], grp=peer)

    def to_groups(make, act):
        @pl.loop(1, groups)
        def _(k):
            act(make((grp + k) % groups))

    def text_first():
        loads[7].wait()

        @pl.loop(0, text_blocks)
        def _(b):
            tstat_x[xi, b] = row_sums(text_ref[b])

        stats_start(x_stats, tstat_x, ts_sem, tr_sem)

    def text_second():
        tstat_z[zi] = stats_sum(x_stats, tstat_x, ts_sem, tr_sem)
        stats_start(z_stats, tstat_z, ts_sem, tr_sem)

    def text_third():
        for k in range(1, 4):
            z_stats(tstat_z, ts_sem, tr_sem, k, False).wait_recv()

        @pl.loop(0, text_blocks)
        def _(b):
            total = (tstat_z[0, b] + tstat_z[1, b]) + (tstat_z[2, b] + tstat_z[3, b])
            inverse = lax.rsqrt(total / features + 1e-05)
            rows = text_ref[b].astype(jnp.float32)
            rows = rows * spread(inverse, rows.shape[1]) * ogain_ref[...]
            thid_ref[b] = rows.astype(jnp.bfloat16)

        thid_copy.start()

    thid_copy = pltpu.make_async_copy(thid_ref, thid_hbm, local_sem.at[0])
    table_smem = pltpu.make_async_copy(table, table_s, local_sem.at[1])
    place_own = pltpu.make_async_copy(table.at[grp], places_ref.at[grp], local_sem.at[2])
    out_own = pltpu.make_async_copy(outbox.at[grp], arrived_ref.at[grp], local_sem.at[3])

    @pl.when(core == 1)
    def _():
        pl.semaphore_wait(turn_sem, 1)

    opened = False
    order = arrival_order()
    handover = 1 + max(n for n, step in enumerate(order) if step[0] == "z" and (step[2] <= 2 or step[2:] in ((3, 0), (3, 1))))
    for n, step in enumerate(order):
        if n == handover:

            @pl.when(core == 0)
            def _():
                pl.semaphore_signal(turn_sem, inc=1, device_id={"grp": grp + 1 - 2 * core}, device_id_type=MESH)

        if step[0] == "own":
            for d in "UD":
                go(z_copy(d, 1, step[1]))
        elif step[0] == "ownx":
            across(0, step[1])
            if step[1] == PIECES - 1:
                to_ranks(start)
        elif step[0] == "task":
            if not opened:
                loads[8].wait()
                opened = True
            project(step[1])
        elif step[0] == "z":
            _, d, age, s = step
            z_arrival(d, age, s).wait_recv()
            if goes_on(d, age, s):
                go(z_copy(d, age + 1, s))
            if age % Z_LO == 0:
                across(plane_of(d, age), s)
        else:
            _, q, d, age, s = step
            source = x_from[d] if age == 1 else x_far
            x_copy(q, source, d, s, xr_sem.at[q, s]).wait_recv()
            if age == 1 and s % 2 == (d == "L"):
                go(x_copy(q, source, d, s, xr_sem.at[q, s]))

    stats_start(x_stats, pstat_x, ps_sem, pr_sem)
    tables()
    pstat_z[zi] = stats_sum(x_stats, pstat_x, ps_sem, pr_sem)
    stats_start(z_stats, pstat_z, ps_sem, pr_sem)
    table_smem.wait()
    for k in range(1, 4):
        z_stats(pstat_z, ps_sem, pr_sem, k, False).wait_recv()

    @pl.loop(0, pstat_z.shape[1])
    def _(b):
        total = (pstat_z[0, b] + pstat_z[1, b]) + (pstat_z[2, b] + pstat_z[3, b])
        inverse = lax.rsqrt(total / features + 1e-05)
        images = LANES // PATCH
        rows = proj[pl.ds(b * images, images)]
        shape = rows.shape
        rows = rows.reshape(LANES, shape[-1]).astype(jnp.float32)
        rows = rows * spread(inverse, shape[-1]) * ogain_ref[...]
        proj[pl.ds(b * images, images)] = rows.astype(jnp.bfloat16).reshape(shape)

    @pl.loop(0, groups)
    def _(o):
        for r in range(CAP):
            outbox[o, r] = proj[table_s[o, 0, CAP + r]]

    @pl.loop(0, groups // 2)
    def _(k):
        out_copy((grp + 1 + k) % groups).start()

        @pl.when(k < groups // 2 - 1)
        def _():
            out_copy((grp + groups - 1 - k) % groups).start()

    out_own.start()
    place_own.start()
    to_groups(table_copy, start)

    text_first()
    text_second()
    text_third()

    to_ranks(wait_send)
    to_groups(table_copy, wait_send)
    for copy in sends:
        copy.wait_send()
    thid_copy.wait()
    place_own.wait()

    @pl.loop(1, groups)
    def _(k):
        peer = (grp + k) % groups
        remote(table.at[peer], places_ref.at[peer], os_sem.at[peer], or_sem.at[peer], grp=peer).wait_recv()

    @pl.loop(1, groups)
    def _(k):
        peer = (grp + k) % groups
        remote(outbox.at[peer], arrived_ref.at[peer], as_sem.at[peer], ar_sem.at[peer], grp=peer).wait()

    out_own.wait()


def overlay_kernel(places_hbm, thid_hbm, arrived_hbm, out_hbm, places_ref, thid_ref, arrived_ref, rows, sem):
    chunks = rows.shape[0]
    blocks = thid_ref.shape[0]
    places_copy = pltpu.make_async_copy(places_hbm, places_ref, sem.at[0])
    arrived_copy = pltpu.make_async_copy(arrived_hbm, arrived_ref, sem.at[1])
    loads = [pltpu.make_async_copy(thid_hbm.at[b], thid_ref.at[b], sem.at[2 + b]) for b in range(blocks)]
    for copy in [places_copy, *loads, arrived_copy]:
        copy.start()
    for b in range(blocks):
        loads[b].wait()
        for c in range(chunks):
            rows[c, b * LANES : (b + 1) * LANES] = thid_ref[b, :, c * LANES : (c + 1) * LANES].astype(jnp.float32)
    places_copy.wait()
    arrived_copy.wait()

    @pl.loop(0, arrived_ref.shape[0])
    def _(g):
        for r in range(CAP):
            at = places_ref[g, 0, r]

            @pl.when(at >= 0)
            def _():
                image = arrived_ref[g, r].astype(jnp.float32)
                for c in range(chunks):
                    rows[c, pl.ds(at, PATCH), :] = image[:, c * LANES : (c + 1) * LANES]

    stores = []
    for b in range(blocks):
        for c in range(chunks):
            thid_ref[b, :, c * LANES : (c + 1) * LANES] = rows[c, b * LANES : (b + 1) * LANES].astype(jnp.bfloat16)
        copy = pltpu.make_async_copy(thid_ref.at[b], out_hbm.at[b], sem.at[2 + b])
        copy.start()
        stores.append(copy)
    for copy in stores:
        copy.wait()


def on_device(
    ranks,
    vis_features,
    vis_gain,
    proj_weight,
    proj_bias,
    text_embed,
    out_gain,
    image_counts,
    owner_block,
    offsets,
):
    groups = lax.axis_size("grp")
    width, columns = proj_weight.shape
    seq_len = text_embed.shape[0]
    slots = ranks * owner_block.shape[0]
    text_blocks = seq_len // LANES
    stat_blocks = slots * PATCH // LANES
    bf16, f32, i32 = jnp.bfloat16, jnp.float32, jnp.int32
    hbm = pl.BlockSpec(memory_space=pltpu.HBM)
    dma = pltpu.SemaphoreType.DMA
    arrived, places, thid = pl.pallas_call(
        functools.partial(exchange_kernel, (groups, ranks, ranks * columns)),
        out_shape=(
            jax.ShapeDtypeStruct((groups, CAP, PATCH, columns), bf16),
            jax.ShapeDtypeStruct((groups, 1, LANES), i32),
            jax.ShapeDtypeStruct((text_blocks, LANES, columns), bf16),
        ),
        in_specs=[hbm] * 9,
        out_specs=(pl.BlockSpec(memory_space=pl.ANY),) * 3,
        scratch_shapes=[
            pltpu.VMEM(vis_features.shape, bf16),
            pltpu.VMEM((width,), f32),
            pltpu.VMEM((columns,), f32),
            pltpu.VMEM((columns,), f32),
            pltpu.SMEM(image_counts.shape, i32),
            pltpu.SMEM(owner_block.shape, i32),
            pltpu.SMEM(offsets.shape, i32),
            pltpu.VMEM((ranks, PIECES, PATCH, width), bf16),
            pltpu.VMEM((2, 2 * Z_LO - 2, PIECES, PATCH, width), bf16),
            pltpu.VMEM((width, columns), bf16),
            pltpu.VMEM((text_blocks, LANES, columns), bf16),
            pltpu.VMEM((text_blocks, LANES, columns), bf16),
            pltpu.VMEM((slots, PATCH, columns), bf16),
            pltpu.VMEM((groups, CAP, PATCH, columns), bf16),
            pltpu.VMEM((ranks, 1, LANES), i32),
            pltpu.VMEM((groups, 1, LANES), i32),
            pltpu.SMEM((groups, 1, LANES), i32),
            pltpu.VMEM((DP_X, text_blocks, 1, LANES), f32),
            pltpu.VMEM((DP_Z, text_blocks, 1, LANES), f32),
            pltpu.VMEM((DP_X, stat_blocks, 1, LANES), f32),
            pltpu.VMEM((DP_Z, stat_blocks, 1, LANES), f32),
            dma((13,)),
            dma((2, 2 * Z_LO, PIECES)),
            dma((2, 2 * Z_LO, PIECES)),
            dma((DP_Z, 2, PIECES)),
            dma((DP_Z, PIECES)),
            dma((ranks, PIECES)),
            dma((ranks,)),
            dma((ranks,)),
            dma((DP_X + DP_Z,)),
            dma((DP_X + DP_Z,)),
            dma((DP_X + DP_Z,)),
            dma((DP_X + DP_Z,)),
            dma((groups,)),
            dma((groups,)),
            dma((groups,)),
            dma((groups,)),
            pltpu.SemaphoreType.REGULAR,
        ],
        compiler_params=pltpu.CompilerParams(
            collective_id=0, has_side_effects=True, vmem_limit_bytes=60 << 20
        ),
        name="exchange",
    )(
        vis_features,
        vis_gain,
        proj_weight,
        proj_bias,
        text_embed.reshape(text_blocks, LANES, columns),
        out_gain,
        image_counts,
        owner_block,
        offsets,
    )
    hidden = pl.pallas_call(
        overlay_kernel,
        out_shape=jax.ShapeDtypeStruct((text_blocks, LANES, columns), bf16),
        in_specs=[hbm] * 3,
        out_specs=pl.BlockSpec(memory_space=pl.ANY),
        scratch_shapes=[
            pltpu.SMEM((groups, 1, LANES), i32),
            pltpu.VMEM((text_blocks, LANES, columns), bf16),
            pltpu.VMEM((groups, CAP, PATCH, columns), bf16),
            pltpu.VMEM((columns // LANES, seq_len, LANES), f32),
            dma((2 + text_blocks,)),
        ],
        compiler_params=pltpu.CompilerParams(vmem_limit_bytes=60 << 20),
        name="overlay",
    )(places, thid, arrived)
    return hidden.reshape(seq_len, columns)


def solution(mesh):
    return jax.shard_map(
        functools.partial(on_device, mesh.shape["dp"]),
        mesh=mesh,
        in_specs=(
            P(("grp", "dp"), None),
            P(),
            P(None, "dp"),
            P("dp"),
            P("grp", "dp"),
            P("dp"),
            P(("grp", "dp")),
            P(("grp", "dp")),
            P(("grp", "dp")),
        ),
        out_specs=P("grp", "dp"),
        check_vma=False,
    )
```
